32 devices in a mesh: groups: 2 (over x), dates: 16 (over z, y, core).
Axes of the slice: x: 2, y: 2, z: 4, core: 2. Of those that a mesh axis runs over, the one named last changes fastest.
Arguments:
- scenes: bfloat16 [64, 16, 7, 256], P(('groups', 'dates')), parts along dimension 0, as said below
- quality: bfloat16 [64, 16, 256], P(('groups', 'dates')), parts along dimension 0, may hold values from 0.099609375 to 1
- pif_mask: float32 [32, 256], P(('groups', 'dates')), parts along dimension 0, may hold values from 0.05 to 1
- counts: int32 [32], P(('groups', 'dates')), parts along dimension 0, may hold values from 1 to 32, as said below
Outputs:
- normalized: bfloat16 [64, 16, 7, 256], P(('groups', 'dates')), parts along dimension 0
The draws below stay inside these ranges and needn't reach their ends.
There are 2 independent parts, one for each index of `groups`. The reference program is written for one: setup_inputs(seed, part) draws one part's arguments, and reference() takes and returns one part's arrays. A program takes and returns all parts, laid end to end along the dimension named above; each array names one. Nothing has to cross between parts.
Inputs may be any that keep to these rules, and one draw needn't show every extreme that they name: Tile t is valid on dates 0 to counts[t] - 1; some tile is valid on all 32 dates. scenes are finite reflectances.
All inputs are finite; a program needn't handle non-finite values.
Results may differ from the reference program's by a relative error of at most 0.0005.
Values may be sent and summed in bfloat16 or wider, within the bound.
A program may use at most 64 MiB of HBM per device.

```python
import math
import jax
import jax.numpy as jnp
from jax import lax

BANDS = 7
PIX = 256
DATES = 32
TILES = 16


def draw_scenes(key, part):
    keys = jax.random.split(jax.random.fold_in(key, 11), 4)
    surface = jax.random.normal(keys[0], (TILES, BANDS, PIX), jnp.float32)
    date_gain = jax.random.uniform(keys[1], (DATES, BANDS), jnp.float32, 0.6, 1.6)
    date_shift = 0.5 * jax.random.normal(keys[2], (DATES, BANDS), jnp.float32)
    noise = 0.3 * jax.random.normal(keys[3], (DATES, TILES, BANDS, PIX), jnp.float32)
    values = surface[None] * date_gain[:, None, :, None] + date_shift[:, None, :, None] + noise
    return values.astype(jnp.bfloat16)


def draw_counts(key, part):
    keys = jax.random.split(jax.random.fold_in(key, 23), 3)
    first = jax.random.randint(keys[0], (TILES,), 0, DATES)
    second = jax.random.randint(keys[1], (TILES,), 0, DATES)
    valid = 1 + first * second // DATES
    where = jax.random.randint(keys[2], (), 0, TILES)
    return valid.at[where].set(DATES).astype(jnp.int32)


def steps_of(stream_key, dims, shards, smallest, largest):
    def one(axis_at, blocks):
        heights = jax.random.uniform(jax.random.fold_in(jax.random.fold_in(stream_key, 6), axis_at), (blocks,), jnp.float32, smallest / len(shards), largest / len(shards))
        return jnp.repeat(jnp.exp(heights), dims[axis_at] // blocks).reshape((-1,) + (1,) * (len(dims) - axis_at - 1))

    level = one(*shards[0])
    for cut in shards[1:]:
        level = level * one(*cut)
    return level


def setup_inputs(seed: int = 0, part: int = 0) -> dict:
    arg_keys = jax.random.split(jax.random.key(seed), 5)
    part_keys = jax.random.split(jax.random.fold_in(arg_keys[4], part), 5)
    return {
        "scenes": draw_scenes(jax.random.fold_in(jax.random.fold_in(arg_keys[4], part), 71), part),
        "quality": jnp.clip(0.099609375 + 0.9003906 * jax.random.uniform(part_keys[1], (DATES, TILES, PIX), jnp.float32) ** steps_of(part_keys[1], (DATES, TILES, PIX), ((0, 16),), -0.2, 0.2), 0.099609375, 1.0).astype(jnp.bfloat16),
        "pif_mask": jnp.clip(jnp.exp(math.log(1.0) - 2.9957323 * jax.random.uniform(part_keys[2], (TILES, PIX), jnp.float32) ** steps_of(part_keys[2], (TILES, PIX), ((0, 16),), -0.2, 0.2)), 0.05, 1.0),
        "counts": draw_counts(jax.random.fold_in(jax.random.fold_in(arg_keys[4], part), 71), part),
    }


def solve_fit(weight_sum, sum_x, sum_xx, sum_y, sum_xy):
    total = weight_sum[:, None]
    mean_x = sum_x / total
    mean_y = sum_y / total
    spread = sum_xx / total - mean_x * mean_x + 1e-5
    gain = (sum_xy / total - mean_x * mean_y) / spread
    return gain, mean_y - gain * mean_x


def reference(scenes, quality, pif_mask, counts):
    date_ids = jnp.arange(DATES, dtype=jnp.int32)
    covered = (date_ids[:, None] < counts[None, :]).astype(jnp.float32)

    def accumulate(carry, item):
        weighted, totals = carry
        scene, qual, cover = item
        weight = qual.astype(jnp.float32) * cover[:, None]
        return (weighted + weight[:, None, :] * scene.astype(jnp.float32), totals + weight), None

    start = (jnp.zeros((TILES, BANDS, PIX), jnp.float32), jnp.zeros((TILES, PIX), jnp.float32))
    (weighted, totals), _ = lax.scan(accumulate, start, (scenes, quality, covered))
    composite = weighted / totals[:, None, :]

    def partials(item):
        scene, qual, cover = item
        fit = qual.astype(jnp.float32) * cover[:, None] * pif_mask
        values = scene.astype(jnp.float32)
        fitted = fit[:, None, :] * values
        return (jnp.sum(fit), jnp.sum(fitted, axis=(0, 2)), jnp.sum(fitted * values, axis=(0, 2)),
                jnp.sum(fit[:, None, :] * composite, axis=(0, 2)), jnp.sum(fitted * composite, axis=(0, 2)))

    weight_sum, sum_x, sum_xx, sum_y, sum_xy = lax.map(partials, (scenes, quality, covered))
    gain, offset = solve_fit(weight_sum, sum_x, sum_xx, sum_y, sum_xy)

    def apply_fit(item):
        scene, slope, shift = item
        return (slope[None, :, None] * scene.astype(jnp.float32) + shift[None, :, None]).astype(jnp.bfloat16)

    return lax.map(apply_fit, (scenes, gain, offset))
```

```python
import functools

import jax
import jax.numpy as jnp
from jax import lax
from jax.experimental import pallas as pl
from jax.experimental.pallas import tpu as pltpu
from jax.sharding import PartitionSpec as P

AXIS = "dates"
LANES = 128


def fused(n, scenes_hbm, quality_hbm, mask_hbm, counts_ref, out_ref,
          own, own_q, q_rows, mask, stage, recv, fitted, part, got,
          local_sem, send_a, recv_a, send_b, recv_b):
    dates, tiles, bands, pix = own.shape
    mine = tiles // n
    rows = bands + 1
    me = lax.axis_index(AXIS)

    barrier = pltpu.get_barrier_semaphore()

    def greet(k, carry):
        pl.semaphore_signal(barrier, inc=1, device_id={AXIS: lax.rem(me + k, n)})
        return carry

    lax.fori_loop(1, n, greet, 0)
    loads = [
        pltpu.make_async_copy(quality_hbm, own_q, local_sem.at[0]),
        pltpu.make_async_copy(scenes_hbm, own, local_sem.at[1]),
        pltpu.make_async_copy(mask_hbm, mask, local_sem.at[2]),
    ]
    for load in loads:
        load.start()
    for load in loads:
        load.wait()

    q_rows[...] = own_q[...].astype(jnp.float32)

    def stage_tile(t, carry):
        for i in range(dates):
            block = jnp.concatenate(
                [own[i, t].astype(jnp.float32), q_rows[i, pl.ds(t, 1), :]], axis=0
            )
            stage[t, i] = block.astype(jnp.bfloat16)
        return carry

    lax.fori_loop(0, tiles, stage_tile, 0, unroll=min(tiles, 16))
    recv[me] = stage[pl.ds(me * mine, mine)]

    pl.semaphore_wait(barrier, n - 1)

    def block_copy(k):
        peer = lax.rem(me + k, n)
        return pltpu.make_async_remote_copy(
            src_ref=stage.at[pl.ds(peer * mine, mine)],
            dst_ref=recv.at[me],
            send_sem=send_a.at[peer],
            recv_sem=recv_a.at[me],
            device_id={AXIS: peer},
        )

    def block_arrival(source):
        return pltpu.make_async_remote_copy(
            src_ref=stage.at[pl.ds(source * mine, mine)],
            dst_ref=recv.at[source],
            send_sem=send_a.at[source],
            recv_sem=recv_a.at[source],
            device_id={AXIS: source},
        )

    def send_block(k, carry):
        block_copy(k).start()
        return carry

    lax.fori_loop(1, n, send_block, 0)

    last_row = lax.broadcasted_iota(jnp.int32, (rows, pix), 0) == bands
    lane = lax.broadcasted_iota(jnp.int32, (rows, LANES), 1)

    def lane_sum(values):
        return jnp.sum(values, axis=1, keepdims=True)

    def take(source, totals):
        totals = list(totals)
        sums = jnp.zeros((rows, LANES), jnp.float32)
        for i in range(dates):
            sum_x = sum_xx = 0.0
            for t in range(mine):
                block = recv[source, t, i].astype(jnp.float32)
                covered = jnp.where(source * dates + i < counts_ref[t], 1.0, 0.0)
                weight = block[bands:] * covered
                values = jnp.where(last_row, 1.0, block)
                weighted = weight * values
                totals[t] = totals[t] + weighted
                fit_x = weighted * mask[t:t + 1, :]
                fitted[source, t, i] = fit_x
                sum_x = sum_x + fit_x
                sum_xx = sum_xx + fit_x * values
            sums = jnp.where(lane == 4 * i, lane_sum(sum_x), sums)
            sums = jnp.where(lane == 4 * i + 1, lane_sum(sum_xx), sums)
        part[source] = sums
        return tuple(totals)

    totals = tuple(jnp.zeros((rows, pix), jnp.float32) for _ in range(mine))
    totals = take(me, totals)

    def take_arrival(k, totals):
        source = lax.rem(me - k + n, n)
        block_arrival(source).wait_recv()
        return take(source, totals)

    totals = lax.fori_loop(1, n, take_arrival, totals)
    composite = [total / total[bands:] for total in totals]

    def finish(source):
        sums = part[source]
        for i in range(dates):
            sum_y = sum_xy = 0.0
            for t in range(mine):
                fit_x = fitted[source, t, i]
                sum_y = sum_y + fit_x[bands:] * composite[t]
                sum_xy = sum_xy + fit_x * composite[t]
            sums = jnp.where(lane == 4 * i + 2, lane_sum(sum_y), sums)
            sums = jnp.where(lane == 4 * i + 3, lane_sum(sum_xy), sums)
        part[source] = sums

    def finish_peer(k, carry):
        finish(lax.rem(me + k, n))
        return carry

    lax.fori_loop(0, n, finish_peer, 0, unroll=min(n, 16))
    got[me] = part[me]

    def sums_copy(k):
        peer = lax.rem(me + k, n)
        return pltpu.make_async_remote_copy(
            src_ref=part.at[peer],
            dst_ref=got.at[me],
            send_sem=send_b.at[peer],
            recv_sem=recv_b.at[me],
            device_id={AXIS: peer},
        )

    def send_sums(k, carry):
        sums_copy(k).start()
        return carry

    lax.fori_loop(1, n, send_sums, 0)

    def take_sums(k, total):
        source = lax.rem(me - k + n, n)
        pltpu.make_async_remote_copy(
            src_ref=part.at[source],
            dst_ref=got.at[source],
            send_sem=send_b.at[source],
            recv_sem=recv_b.at[source],
            device_id={AXIS: source},
        ).wait_recv()
        return total + got[source]

    sums = lax.fori_loop(1, n, take_sums, got[me])
    lines = []
    for i in range(dates):
        sum_x, sum_xx, sum_y, sum_xy = (sums[:, 4 * i + s:4 * i + s + 1] for s in range(4))
        total = sum_x[bands:]
        mean_x = sum_x / total
        mean_y = sum_y / total
        spread = sum_xx / total - mean_x * mean_x + 1e-5
        gain = (sum_xy / total - mean_x * mean_y) / spread
        offset = mean_y - gain * mean_x
        lines.append((
            jnp.broadcast_to(gain[:bands], (bands, pix)),
            jnp.broadcast_to(offset[:bands], (bands, pix)),
        ))

    def apply(t, carry):
        for i in range(dates):
            gain, offset = lines[i]
            out_ref[i, t] = (gain * own[i, t].astype(jnp.float32) + offset).astype(out_ref.dtype)
        return carry

    lax.fori_loop(0, tiles, apply, 0, unroll=min(tiles, 16))

    def drain(k, carry):
        block_copy(k).wait_send()
        sums_copy(k).wait_send()
        return carry

    lax.fori_loop(1, n, drain, 0)


def local(n, scenes, quality, pif_mask, counts):
    dates, tiles, bands, pix = scenes.shape
    mine = tiles // n
    rows = bands + 1
    anywhere = pl.BlockSpec(memory_space=pl.ANY)
    return pl.pallas_call(
        functools.partial(fused, n),
        out_shape=jax.ShapeDtypeStruct(scenes.shape, scenes.dtype),
        in_specs=[anywhere, anywhere, anywhere, pl.BlockSpec(memory_space=pltpu.SMEM)],
        out_specs=pl.BlockSpec(memory_space=pltpu.VMEM),
        scratch_shapes=[
            pltpu.VMEM(scenes.shape, scenes.dtype),
            pltpu.VMEM(quality.shape, quality.dtype),
            pltpu.VMEM(quality.shape, jnp.float32),
            pltpu.VMEM(pif_mask.shape, jnp.float32),
            pltpu.VMEM((tiles, dates, rows, pix), scenes.dtype),
            pltpu.VMEM((n, mine, dates, rows, pix), scenes.dtype),
            pltpu.VMEM((n, mine, dates, rows, pix), jnp.float32),
            pltpu.VMEM((n, rows, LANES), jnp.float32),
            pltpu.VMEM((n, rows, LANES), jnp.float32),
            pltpu.SemaphoreType.DMA((3,)),
            pltpu.SemaphoreType.DMA((n,)),
            pltpu.SemaphoreType.DMA((n,)),
            pltpu.SemaphoreType.DMA((n,)),
            pltpu.SemaphoreType.DMA((n,)),
        ],
        compiler_params=pltpu.CompilerParams(collective_id=0, has_side_effects=True),
    )(scenes, quality, pif_mask, counts)


def solution(mesh):
    both = ("groups", AXIS)
    placed = (P(both, None, None, None), P(both, None, None), P(both, None), P(both))
    return jax.shard_map(
        functools.partial(local, mesh.shape[AXIS]),
        mesh=mesh,
        in_specs=placed,
        out_specs=placed[0],
        check_vma=False,
    )
```

```python
import functools

import jax
import jax.numpy as jnp
from jax import lax
from jax.experimental import pallas as pl
from jax.experimental.pallas import tpu as pltpu
from jax.sharding import PartitionSpec as P

AXIS = "dates"
LANES = 128


def fused(n, scenes_hbm, quality_hbm, mask_hbm, counts_ref, out_ref,
          own, own_q, wide, mask, stage, recv, fitted, part, got,
          local_sem, send_a, recv_a, send_b, recv_b):
    dates, bands, tiles, pix = own.shape
    mine = tiles // n
    rows, halves = bands + 1, pix // LANES
    me = lax.axis_index(AXIS)

    barrier = pltpu.get_barrier_semaphore()

    def greet(k, carry):
        pl.semaphore_signal(barrier, inc=1, device_id={AXIS: lax.rem(me + k, n)})
        return carry

    lax.fori_loop(1, n, greet, 0)
    loads = [
        pltpu.make_async_copy(quality_hbm, own_q, local_sem.at[0]),
        pltpu.make_async_copy(scenes_hbm, own, local_sem.at[1]),
        pltpu.make_async_copy(mask_hbm, mask, local_sem.at[2]),
    ]
    for load in loads:
        load.start()
    for load in loads:
        load.wait()

    for i in range(dates):
        for h in range(halves):
            columns = slice(h * LANES, (h + 1) * LANES)
            for b in range(bands):
                wide[i, h, b * tiles:(b + 1) * tiles] = own[i, b, :, columns].astype(jnp.float32)
            wide[i, h, bands * tiles:] = own_q[i, :, columns].astype(jnp.float32)

    def stage_tile(t, carry):
        for i in range(dates):
            for h in range(halves):
                block = wide[i, h, pl.ds(t, rows, stride=tiles), :]
                stage[t, i, :, h * LANES:(h + 1) * LANES] = block.astype(jnp.bfloat16)
        return carry

    lax.fori_loop(0, tiles, stage_tile, 0, unroll=min(tiles, 16))
    recv[me] = stage[pl.ds(me * mine, mine)]

    pl.semaphore_wait(barrier, n - 1)

    def block_copy(k):
        peer = lax.rem(me + k, n)
        return pltpu.make_async_remote_copy(
            src_ref=stage.at[pl.ds(peer * mine, mine)],
            dst_ref=recv.at[me],
            send_sem=send_a.at[peer],
            recv_sem=recv_a.at[me],
            device_id={AXIS: peer},
        )

    def block_arrival(source):
        return pltpu.make_async_remote_copy(
            src_ref=stage.at[pl.ds(source * mine, mine)],
            dst_ref=recv.at[source],
            send_sem=send_a.at[source],
            recv_sem=recv_a.at[source],
            device_id={AXIS: source},
        )

    def send_block(k, carry):
        block_copy(k).start()
        return carry

    lax.fori_loop(1, n, send_block, 0)

    last_row = lax.broadcasted_iota(jnp.int32, (rows, pix), 0) == bands
    lane = lax.broadcasted_iota(jnp.int32, (rows, LANES), 1)

    def lane_sum(values):
        return jnp.sum(values, axis=1, keepdims=True)

    def take(source, totals):
        totals = list(totals)
        sums = jnp.zeros((rows, LANES), jnp.float32)
        for i in range(dates):
            sum_x = sum_xx = 0.0
            for t in range(mine):
                block = recv[source, t, i].astype(jnp.float32)
                covered = jnp.where(source * dates + i < counts_ref[t], 1.0, 0.0)
                weight = block[bands:] * covered
                values = jnp.where(last_row, 1.0, block)
                weighted = weight * values
                totals[t] = totals[t] + weighted
                fit_x = weighted * mask[t:t + 1, :]
                fitted[source, t, i] = fit_x
                sum_x = sum_x + fit_x
                sum_xx = sum_xx + fit_x * values
            sums = jnp.where(lane == 4 * i, lane_sum(sum_x), sums)
            sums = jnp.where(lane == 4 * i + 1, lane_sum(sum_xx), sums)
        part[source] = sums
        return tuple(totals)

    totals = tuple(jnp.zeros((rows, pix), jnp.float32) for _ in range(mine))
    totals = take(me, totals)

    def take_arrival(k, totals):
        source = lax.rem(me - k + n, n)
        block_arrival(source).wait_recv()
        return take(source, totals)

    totals = lax.fori_loop(1, n, take_arrival, totals)
    composite = [total / total[bands:] for total in totals]

    def finish(source):
        sums = part[source]
        for i in range(dates):
            sum_y = sum_xy = 0.0
            for t in range(mine):
                fit_x = fitted[source, t, i]
                sum_y = sum_y + fit_x[bands:] * composite[t]
                sum_xy = sum_xy + fit_x * composite[t]
            sums = jnp.where(lane == 4 * i + 2, lane_sum(sum_y), sums)
            sums = jnp.where(lane == 4 * i + 3, lane_sum(sum_xy), sums)
        part[source] = sums

    def finish_peer(k, carry):
        finish(lax.rem(me + k, n))
        return carry

    lax.fori_loop(0, n, finish_peer, 0, unroll=min(n, 16))
    got[me] = part[me]

    def sums_copy(k):
        peer = lax.rem(me + k, n)
        return pltpu.make_async_remote_copy(
            src_ref=part.at[peer],
            dst_ref=got.at[me],
            send_sem=send_b.at[peer],
            recv_sem=recv_b.at[me],
            device_id={AXIS: peer},
        )

    def send_sums(k, carry):
        sums_copy(k).start()
        return carry

    lax.fori_loop(1, n, send_sums, 0)

    def take_sums(k, total):
        source = lax.rem(me - k + n, n)
        pltpu.make_async_remote_copy(
            src_ref=part.at[source],
            dst_ref=got.at[source],
            send_sem=send_b.at[source],
            recv_sem=recv_b.at[source],
            device_id={AXIS: source},
        ).wait_recv()
        return total + got[source]

    sums = lax.fori_loop(1, n, take_sums, got[me])
    for i in range(dates):
        sum_x, sum_xx, sum_y, sum_xy = (sums[:, 4 * i + s:4 * i + s + 1] for s in range(4))
        total = sum_x[bands:]
        mean_x = sum_x / total
        mean_y = sum_y / total
        spread = sum_xx / total - mean_x * mean_x + 1e-5
        gain = (sum_xy / total - mean_x * mean_y) / spread
        offset = mean_y - gain * mean_x
        gain = jnp.broadcast_to(gain, (rows, LANES))
        offset = jnp.broadcast_to(offset, (rows, LANES))
        for b in range(bands):
            for h in range(halves):
                values = wide[i, h, b * tiles:(b + 1) * tiles]
                scaled = gain[b:b + 1] * values + offset[b:b + 1]
                out_ref[i, b, :, h * LANES:(h + 1) * LANES] = scaled.astype(out_ref.dtype)

    def drain(k, carry):
        block_copy(k).wait_send()
        sums_copy(k).wait_send()
        return carry

    lax.fori_loop(1, n, drain, 0)


def local(n, scenes, quality, pif_mask, counts):
    scenes = scenes.transpose(0, 2, 1, 3)
    dates, bands, tiles, pix = scenes.shape
    mine = tiles // n
    rows = bands + 1
    anywhere = pl.BlockSpec(memory_space=pl.ANY)
    out = pl.pallas_call(
        functools.partial(fused, n),
        out_shape=jax.ShapeDtypeStruct(scenes.shape, scenes.dtype),
        in_specs=[anywhere, anywhere, anywhere, pl.BlockSpec(memory_space=pltpu.SMEM)],
        out_specs=pl.BlockSpec(memory_space=pltpu.VMEM),
        scratch_shapes=[
            pltpu.VMEM(scenes.shape, scenes.dtype),
            pltpu.VMEM(quality.shape, quality.dtype),
            pltpu.VMEM((dates, pix // LANES, rows * tiles, LANES), jnp.float32),
            pltpu.VMEM(pif_mask.shape, jnp.float32),
            pltpu.VMEM((tiles, dates, rows, pix), scenes.dtype),
            pltpu.VMEM((n, mine, dates, rows, pix), scenes.dtype),
            pltpu.VMEM((n, mine, dates, rows, pix), jnp.float32),
            pltpu.VMEM((n, rows, LANES), jnp.float32),
            pltpu.VMEM((n, rows, LANES), jnp.float32),
            pltpu.SemaphoreType.DMA((3,)),
            pltpu.SemaphoreType.DMA((n,)),
            pltpu.SemaphoreType.DMA((n,)),
            pltpu.SemaphoreType.DMA((n,)),
            pltpu.SemaphoreType.DMA((n,)),
        ],
        compiler_params=pltpu.CompilerParams(collective_id=0, has_side_effects=True),
    )(scenes, quality, pif_mask, counts)
    return out.transpose(0, 2, 1, 3)


def solution(mesh):
    both = ("groups", AXIS)
    placed = (P(both, None, None, None), P(both, None, None), P(both, None), P(both))
    return jax.shard_map(
        functools.partial(local, mesh.shape[AXIS]),
        mesh=mesh,
        in_specs=placed,
        out_specs=placed[0],
        check_vma=False,
    )
```

```python
import functools

import jax
import jax.numpy as jnp
from jax import lax
from jax.experimental import pallas as pl
from jax.experimental.pallas import tpu as pltpu
from jax.sharding import PartitionSpec as P

AXIS = "dates"
LANES = 128


def fused(n, scenes_hbm, quality_hbm, mask_hbm, counts_hbm, out_ref,
          own, own_q, wide, mask, counts_ref, stage, recv, fitted, part, got,
          local_sem, send_a, recv_a, send_b, recv_b):
    dates, bands, tiles, pix = own.shape
    mine = tiles // n
    rows, halves = bands + 1, pix // LANES
    me = lax.axis_index(AXIS)

    barrier = pltpu.get_barrier_semaphore()

    def greet(k, carry):
        pl.semaphore_signal(barrier, inc=1, device_id={AXIS: lax.rem(me + k, n)})
        return carry

    lax.fori_loop(1, n, greet, 0)
    loads = [
        pltpu.make_async_copy(quality_hbm, own_q, local_sem.at[0]),
        pltpu.make_async_copy(scenes_hbm, own, local_sem.at[1]),
        pltpu.make_async_copy(mask_hbm, mask, local_sem.at[2]),
        pltpu.make_async_copy(counts_hbm, counts_ref, local_sem.at[3]),
    ]
    for load in loads:
        load.start()
    for load in loads:
        load.wait()

    for i in range(dates):
        for h in range(halves):
            columns = slice(h * LANES, (h + 1) * LANES)
            for b in range(bands):
                wide[i, h, b * tiles:(b + 1) * tiles] = own[i, b, :, columns].astype(jnp.float32)
            wide[i, h, bands * tiles:] = own_q[i, :, columns].astype(jnp.float32)

    def stage_tile(t, carry):
        for i in range(dates):
            for h in range(halves):
                block = wide[i, h, pl.ds(t, rows, stride=tiles), :]
                stage[t, i, :, h * LANES:(h + 1) * LANES] = block.astype(jnp.bfloat16)
        return carry

    lax.fori_loop(0, tiles, stage_tile, 0, unroll=min(tiles, 16))
    recv[me] = stage[pl.ds(me * mine, mine)]

    pl.semaphore_wait(barrier, n - 1)

    def block_copy(k):
        peer = lax.rem(me + k, n)
        return pltpu.make_async_remote_copy(
            src_ref=stage.at[pl.ds(peer * mine, mine)],
            dst_ref=recv.at[me],
            send_sem=send_a.at[peer],
            recv_sem=recv_a.at[me],
            device_id={AXIS: peer},
        )

    def block_arrival(source):
        return pltpu.make_async_remote_copy(
            src_ref=stage.at[pl.ds(source * mine, mine)],
            dst_ref=recv.at[source],
            send_sem=send_a.at[source],
            recv_sem=recv_a.at[source],
            device_id={AXIS: source},
        )

    def send_block(k, carry):
        block_copy(k).start()
        return carry

    lax.fori_loop(1, n, send_block, 0)

    last_row = lax.broadcasted_iota(jnp.int32, (rows, pix), 0) == bands
    lane = lax.broadcasted_iota(jnp.int32, (rows, LANES), 1)

    def lane_sum(values):
        return jnp.sum(values, axis=1, keepdims=True)

    def take(source, totals):
        totals = list(totals)
        sums = jnp.zeros((rows, LANES), jnp.float32)
        for i in range(dates):
            sum_x = sum_xx = 0.0
            for t in range(mine):
                block = recv[source, t, i].astype(jnp.float32)
                covered = jnp.where(source * dates + i < counts_ref[t], 1.0, 0.0)
                weight = block[bands:] * covered
                values = jnp.where(last_row, 1.0, block)
                weighted = weight * values
                totals[t] = totals[t] + weighted
                fit_x = weighted * mask[t:t + 1, :]
                fitted[source, t, i] = fit_x
                sum_x = sum_x + fit_x
                sum_xx = sum_xx + fit_x * values
            sums = jnp.where(lane == 4 * i, lane_sum(sum_x), sums)
            sums = jnp.where(lane == 4 * i + 1, lane_sum(sum_xx), sums)
        part[source] = sums
        return tuple(totals)

    totals = tuple(jnp.zeros((rows, pix), jnp.float32) for _ in range(mine))
    totals = take(me, totals)

    def take_arrival(k, totals):
        source = lax.rem(me - k + n, n)
        block_arrival(source).wait_recv()
        return take(source, totals)

    totals = lax.fori_loop(1, n, take_arrival, totals)
    composite = [total / total[bands:] for total in totals]

    def finish(source):
        sums = part[source]
        for i in range(dates):
            sum_y = sum_xy = 0.0
            for t in range(mine):
                fit_x = fitted[source, t, i]
                sum_y = sum_y + fit_x[bands:] * composite[t]
                sum_xy = sum_xy + fit_x * composite[t]
            sums = jnp.where(lane == 4 * i + 2, lane_sum(sum_y), sums)
            sums = jnp.where(lane == 4 * i + 3, lane_sum(sum_xy), sums)
        part[source] = sums

    def finish_peer(k, carry):
        finish(lax.rem(me + k, n))
        return carry

    lax.fori_loop(0, n, finish_peer, 0, unroll=min(n, 16))
    got[me] = part[me]

    def sums_copy(k):
        peer = lax.rem(me + k, n)
        return pltpu.make_async_remote_copy(
            src_ref=part.at[peer],
            dst_ref=got.at[me],
            send_sem=send_b.at[peer],
            recv_sem=recv_b.at[me],
            device_id={AXIS: peer},
        )

    def send_sums(k, carry):
        sums_copy(k).start()
        return carry

    lax.fori_loop(1, n, send_sums, 0)

    def take_sums(k, total):
        source = lax.rem(me - k + n, n)
        pltpu.make_async_remote_copy(
            src_ref=part.at[source],
            dst_ref=got.at[source],
            send_sem=send_b.at[source],
            recv_sem=recv_b.at[source],
            device_id={AXIS: source},
        ).wait_recv()
        return total + got[source]

    sums = lax.fori_loop(1, n, take_sums, got[me])
    for i in range(dates):
        sum_x, sum_xx, sum_y, sum_xy = (sums[:, 4 * i + s:4 * i + s + 1] for s in range(4))
        total = sum_x[bands:]
        mean_x = sum_x / total
        mean_y = sum_y / total
        spread = sum_xx / total - mean_x * mean_x + 1e-5
        gain = (sum_xy / total - mean_x * mean_y) / spread
        offset = mean_y - gain * mean_x
        gain = jnp.broadcast_to(gain, (rows, LANES))
        offset = jnp.broadcast_to(offset, (rows, LANES))
        for b in range(bands):
            for h in range(halves):
                values = wide[i, h, b * tiles:(b + 1) * tiles]
                scaled = gain[b:b + 1] * values + offset[b:b + 1]
                out_ref[i, b, :, h * LANES:(h + 1) * LANES] = scaled.astype(out_ref.dtype)

    def drain(k, carry):
        block_copy(k).wait_send()
        sums_copy(k).wait_send()
        return carry

    lax.fori_loop(1, n, drain, 0)


def local(n, scenes, quality, pif_mask, counts):
    scenes = scenes.transpose(0, 2, 1, 3)
    dates, bands, tiles, pix = scenes.shape
    mine = tiles // n
    rows = bands + 1
    in_place = pl.BlockSpec(memory_space=pltpu.HBM)
    out = pl.pallas_call(
        functools.partial(fused, n),
        out_shape=jax.ShapeDtypeStruct(scenes.shape, scenes.dtype),
        in_specs=[in_place] * 4,
        out_specs=pl.BlockSpec(memory_space=pltpu.VMEM),
        scratch_shapes=[
            pltpu.VMEM(scenes.shape, scenes.dtype),
            pltpu.VMEM(quality.shape, quality.dtype),
            pltpu.VMEM((dates, pix // LANES, rows * tiles, LANES), jnp.float32),
            pltpu.VMEM(pif_mask.shape, jnp.float32),
            pltpu.SMEM(counts.shape, jnp.int32),
            pltpu.VMEM((tiles, dates, rows, pix), scenes.dtype),
            pltpu.VMEM((n, mine, dates, rows, pix), scenes.dtype),
            pltpu.VMEM((n, mine, dates, rows, pix), jnp.float32),
            pltpu.VMEM((n, rows, LANES), jnp.float32),
            pltpu.VMEM((n, rows, LANES), jnp.float32),
            pltpu.SemaphoreType.DMA((4,)),
            pltpu.SemaphoreType.DMA((n,)),
            pltpu.SemaphoreType.DMA((n,)),
            pltpu.SemaphoreType.DMA((n,)),
            pltpu.SemaphoreType.DMA((n,)),
        ],
        compiler_params=pltpu.CompilerParams(
            collective_id=0, has_side_effects=True, vmem_limit_bytes=32 * 2**20
        ),
    )(scenes, quality, pif_mask, counts)
    return out.transpose(0, 2, 1, 3)


def solution(mesh):
    both = ("groups", AXIS)
    placed = (P(both, None, None, None), P(both, None, None), P(both, None), P(both))
    return jax.shard_map(
        functools.partial(local, mesh.shape[AXIS]),
        mesh=mesh,
        in_specs=placed,
        out_specs=placed[0],
        check_vma=False,
    )
```

```python
import functools

import jax
import jax.numpy as jnp
from jax import lax
from jax.experimental import pallas as pl
from jax.experimental.pallas import tpu as pltpu
from jax.sharding import PartitionSpec as P

AXIS = "dates"
LANES = 128


def fused(n, scenes_hbm, quality_hbm, mask_hbm, counts_ref, out_ref,
          own, own_q, wide, mask, stage, recv, fitted, part, got,
          local_sem, send_a, recv_a, send_b, recv_b):
    dates, bands, tiles, pix = own.shape
    mine = tiles // n
    rows, halves = bands + 1, pix // LANES
    me = lax.axis_index(AXIS)

    barrier = pltpu.get_barrier_semaphore()

    def greet(k, carry):
        pl.semaphore_signal(barrier, inc=1, device_id={AXIS: lax.rem(me + k, n)})
        return carry

    lax.fori_loop(1, n, greet, 0)
    loads = [
        pltpu.make_async_copy(quality_hbm, own_q, local_sem.at[0]),
        pltpu.make_async_copy(scenes_hbm, own, local_sem.at[1]),
        pltpu.make_async_copy(mask_hbm, mask, local_sem.at[2]),
    ]
    for load in loads:
        load.start()
    for load in loads:
        load.wait()

    for i in range(dates):
        for h in range(halves):
            columns = slice(h * LANES, (h + 1) * LANES)
            for b in range(bands):
                wide[i, h, b * tiles:(b + 1) * tiles] = own[i, b, :, columns].astype(jnp.float32)
            wide[i, h, bands * tiles:] = own_q[i, :, columns].astype(jnp.float32)

    def stage_tile(t, carry):
        for i in range(dates):
            for h in range(halves):
                block = wide[i, h, pl.ds(t, rows, stride=tiles), :]
                stage[t, i, :, h * LANES:(h + 1) * LANES] = block.astype(jnp.bfloat16)
        return carry

    lax.fori_loop(0, tiles, stage_tile, 0, unroll=min(tiles, 16))
    recv[me] = stage[pl.ds(me * mine, mine)]

    pl.semaphore_wait(barrier, n - 1)

    def block_copy(k):
        peer = lax.rem(me + k, n)
        return pltpu.make_async_remote_copy(
            src_ref=stage.at[pl.ds(peer * mine, mine)],
            dst_ref=recv.at[me],
            send_sem=send_a.at[peer],
            recv_sem=recv_a.at[me],
            device_id={AXIS: peer},
        )

    def block_arrival(source):
        return pltpu.make_async_remote_copy(
            src_ref=stage.at[pl.ds(source * mine, mine)],
            dst_ref=recv.at[source],
            send_sem=send_a.at[source],
            recv_sem=recv_a.at[source],
            device_id={AXIS: source},
        )

    def send_block(k, carry):
        block_copy(k).start()
        return carry

    lax.fori_loop(1, n, send_block, 0)

    last_row = lax.broadcasted_iota(jnp.int32, (rows, pix), 0) == bands
    lane = lax.broadcasted_iota(jnp.int32, (rows, LANES), 1)

    def lane_sum(values):
        return jnp.sum(values, axis=1, keepdims=True)

    def take(source, totals):
        totals = list(totals)
        sums = jnp.zeros((rows, LANES), jnp.float32)
        for i in range(dates):
            sum_x = sum_xx = 0.0
            for t in range(mine):
                block = recv[source, t, i].astype(jnp.float32)
                covered = jnp.where(source * dates + i < counts_ref[t], 1.0, 0.0)
                weight = block[bands:] * covered
                values = jnp.where(last_row, 1.0, block)
                weighted = weight * values
                totals[t] = totals[t] + weighted
                fit_x = weighted * mask[t:t + 1, :]
                fitted[source, t, i] = fit_x
                sum_x = sum_x + fit_x
                sum_xx = sum_xx + fit_x * values
            sums = jnp.where(lane == 4 * i, lane_sum(sum_x), sums)
            sums = jnp.where(lane == 4 * i + 1, lane_sum(sum_xx), sums)
        part[source] = sums
        return tuple(totals)

    totals = tuple(jnp.zeros((rows, pix), jnp.float32) for _ in range(mine))
    totals = take(me, totals)

    def take_arrival(k, totals):
        source = lax.rem(me - k + n, n)
        block_arrival(source).wait_recv()
        return take(source, totals)

    totals = lax.fori_loop(1, n, take_arrival, totals)
    composite = [total / total[bands:] for total in totals]

    def finish(source):
        sums = part[source]
        for i in range(dates):
            sum_y = sum_xy = 0.0
            for t in range(mine):
                fit_x = fitted[source, t, i]
                sum_y = sum_y + fit_x[bands:] * composite[t]
                sum_xy = sum_xy + fit_x * composite[t]
            sums = jnp.where(lane == 4 * i + 2, lane_sum(sum_y), sums)
            sums = jnp.where(lane == 4 * i + 3, lane_sum(sum_xy), sums)
        part[source] = sums

    def finish_peer(k, carry):
        finish(lax.rem(me + k, n))
        return carry

    lax.fori_loop(0, n, finish_peer, 0, unroll=min(n, 16))
    got[me] = part[me]

    def sums_copy(k):
        peer = lax.rem(me + k, n)
        return pltpu.make_async_remote_copy(
            src_ref=part.at[peer],
            dst_ref=got.at[me],
            send_sem=send_b.at[peer],
            recv_sem=recv_b.at[me],
            device_id={AXIS: peer},
        )

    def send_sums(k, carry):
        sums_copy(k).start()
        return carry

    lax.fori_loop(1, n, send_sums, 0)

    def take_sums(k, total):
        source = lax.rem(me - k + n, n)
        pltpu.make_async_remote_copy(
            src_ref=part.at[source],
            dst_ref=got.at[source],
            send_sem=send_b.at[source],
            recv_sem=recv_b.at[source],
            device_id={AXIS: source},
        ).wait_recv()
        return total + got[source]

    sums = lax.fori_loop(1, n, take_sums, got[me])
    for i in range(dates):
        sum_x, sum_xx, sum_y, sum_xy = (sums[:, 4 * i + s:4 * i + s + 1] for s in range(4))
        total = sum_x[bands:]
        mean_x = sum_x / total
        mean_y = sum_y / total
        spread = sum_xx / total - mean_x * mean_x + 1e-5
        gain = (sum_xy / total - mean_x * mean_y) / spread
        offset = mean_y - gain * mean_x
        gain = jnp.broadcast_to(gain, (rows, LANES))
        offset = jnp.broadcast_to(offset, (rows, LANES))
        for b in range(bands):
            for h in range(halves):
                values = wide[i, h, b * tiles:(b + 1) * tiles]
                scaled = gain[b:b + 1] * values + offset[b:b + 1]
                out_ref[i, b, :, h * LANES:(h + 1) * LANES] = scaled.astype(out_ref.dtype)

    def drain(k, carry):
        block_copy(k).wait_send()
        sums_copy(k).wait_send()
        return carry

    lax.fori_loop(1, n, drain, 0)


def local(n, scenes, quality, pif_mask, counts):
    scenes = scenes.transpose(0, 2, 1, 3)
    dates, bands, tiles, pix = scenes.shape
    mine = tiles // n
    rows = bands + 1
    in_place = pl.BlockSpec(memory_space=pltpu.HBM)
    out = pl.pallas_call(
        functools.partial(fused, n),
        out_shape=jax.ShapeDtypeStruct(scenes.shape, scenes.dtype),
        in_specs=[in_place] * 3 + [pl.BlockSpec(memory_space=pltpu.SMEM)],
        out_specs=pl.BlockSpec(memory_space=pltpu.VMEM),
        scratch_shapes=[
            pltpu.VMEM(scenes.shape, scenes.dtype),
            pltpu.VMEM(quality.shape, quality.dtype),
            pltpu.VMEM((dates, pix // LANES, rows * tiles, LANES), jnp.float32),
            pltpu.VMEM(pif_mask.shape, jnp.float32),
            pltpu.VMEM((tiles, dates, rows, pix), scenes.dtype),
            pltpu.VMEM((n, mine, dates, rows, pix), scenes.dtype),
            pltpu.VMEM((n, mine, dates, rows, pix), jnp.float32),
            pltpu.VMEM((n, rows, LANES), jnp.float32),
            pltpu.VMEM((n, rows, LANES), jnp.float32),
            pltpu.SemaphoreType.DMA((3,)),
            pltpu.SemaphoreType.DMA((n,)),
            pltpu.SemaphoreType.DMA((n,)),
            pltpu.SemaphoreType.DMA((n,)),
            pltpu.SemaphoreType.DMA((n,)),
        ],
        compiler_params=pltpu.CompilerParams(
            collective_id=0, has_side_effects=True, vmem_limit_bytes=32 * 2**20
        ),
    )(*(pltpu.with_memory_space_constraint(a, pltpu.HBM) for a in (scenes, quality, pif_mask)), counts)
    return out.transpose(0, 2, 1, 3)


def solution(mesh):
    both = ("groups", AXIS)
    placed = (P(both, None, None, None), P(both, None, None), P(both, None), P(both))
    return jax.shard_map(
        functools.partial(local, mesh.shape[AXIS]),
        mesh=mesh,
        in_specs=placed,
        out_specs=placed[0],
        check_vma=False,
    )
```

```python
import functools

import jax
import jax.numpy as jnp
from jax import lax
from jax.experimental import pallas as pl
from jax.experimental.pallas import tpu as pltpu
from jax.sharding import PartitionSpec as P

AXIS = "dates"
LANES = 128


def fused(n, scenes_hbm, quality_hbm, mask_hbm, counts_ref, out_ref,
          own, own_q, wide, mask, stage, recv, fitted, early, part, got,
          local_sem, send_a, recv_a, send_b, recv_b):
    dates, bands, tiles, pix = own.shape
    mine = tiles // n
    rows, halves = bands + 1, pix // LANES
    me = lax.axis_index(AXIS)

    barrier = pltpu.get_barrier_semaphore()

    def greet(k, carry):
        pl.semaphore_signal(barrier, inc=1, device_id={AXIS: lax.rem(me + k, n)})
        return carry

    lax.fori_loop(1, n, greet, 0)
    loads = [
        pltpu.make_async_copy(quality_hbm, own_q, local_sem.at[0]),
        pltpu.make_async_copy(scenes_hbm, own, local_sem.at[1]),
        pltpu.make_async_copy(mask_hbm, mask, local_sem.at[2]),
    ]
    for load in loads:
        load.start()
    for load in loads:
        load.wait()

    for i in range(dates):
        for h in range(halves):
            columns = slice(h * LANES, (h + 1) * LANES)
            for b in range(bands):
                wide[i, h, b * tiles:(b + 1) * tiles] = own[i, b, :, columns].astype(jnp.float32)
            wide[i, h, bands * tiles:] = own_q[i, :, columns].astype(jnp.float32)

    def stage_tile(t, carry):
        for i in range(dates):
            for h in range(halves):
                block = wide[i, h, pl.ds(t, rows, stride=tiles), :]
                stage[t, i, :, h * LANES:(h + 1) * LANES] = block.astype(jnp.bfloat16)
        return carry

    lax.fori_loop(0, tiles, stage_tile, 0, unroll=min(tiles, 16))
    recv[me] = stage[pl.ds(me * mine, mine)]

    pl.semaphore_wait(barrier, n - 1)

    def peer_at(spot):
        step = spot - 1
        half, odd = lax.div(step, 2), lax.rem(step, 2)
        ahead = (1 + half) * (1 - odd) + (n - 1 - half) * odd
        return lax.rem(me + ahead, n)

    def block_copy(peer):
        return pltpu.make_async_remote_copy(
            src_ref=stage.at[pl.ds(peer * mine, mine)],
            dst_ref=recv.at[me],
            send_sem=send_a.at[peer],
            recv_sem=recv_a.at[me],
            device_id={AXIS: peer},
        )

    def block_arrival(source):
        return pltpu.make_async_remote_copy(
            src_ref=stage.at[pl.ds(source * mine, mine)],
            dst_ref=recv.at[source],
            send_sem=send_a.at[source],
            recv_sem=recv_a.at[source],
            device_id={AXIS: source},
        )

    def send_block(k, carry):
        block_copy(peer_at(n - k)).start()
        return carry

    lax.fori_loop(1, n, send_block, 0)

    last_row = lax.broadcasted_iota(jnp.int32, (rows, pix), 0) == bands
    lane = lax.broadcasted_iota(jnp.int32, (rows, LANES), 1)

    def lane_sum(values):
        return jnp.sum(values, axis=1, keepdims=True)

    def take(sources, totals):
        totals = list(totals)
        kept = []
        for source in sources:
            sums = jnp.zeros((rows, LANES), jnp.float32)
            parts = []
            for i in range(dates):
                sum_x = sum_xx = 0.0
                for t in range(mine):
                    block = recv[source, t, i].astype(jnp.float32)
                    covered = jnp.where(source * dates + i < counts_ref[t], 1.0, 0.0)
                    weight = block[bands:] * covered
                    values = jnp.where(last_row, 1.0, block)
                    weighted = weight * values
                    totals[t] = totals[t] + weighted
                    fit_x = weighted * mask[t:t + 1, :]
                    parts.append((t, i, fit_x))
                    sum_x = sum_x + fit_x
                    sum_xx = sum_xx + fit_x * values
                sums = jnp.where(lane == 4 * i, lane_sum(sum_x), sums)
                sums = jnp.where(lane == 4 * i + 1, lane_sum(sum_xx), sums)
            kept.append((source, sums, parts))
        for source, sums, parts in kept:
            early[source] = sums
            for t, i, fit_x in parts:
                fitted[source, t, i] = fit_x
        return tuple(totals)

    batch = 4 if n % 4 == 0 else 1
    totals = tuple(jnp.zeros((rows, pix), jnp.float32) for _ in range(mine))
    first = [peer_at(spot) for spot in range(1, batch)]
    for source in first:
        block_arrival(source).wait_recv()
    totals = take([me] + first, totals)

    def take_batch(g, totals):
        sources = [peer_at(g * batch + r) for r in range(batch)]
        for source in sources:
            block_arrival(source).wait_recv()
        return take(sources, totals)

    totals = lax.fori_loop(1, n // batch, take_batch, totals)
    composite = [total / total[bands:] for total in totals]

    def finish(source):
        sums = early[source]
        for i in range(dates):
            sum_y = sum_xy = 0.0
            for t in range(mine):
                fit_x = fitted[source, t, i]
                sum_y = sum_y + fit_x[bands:] * composite[t]
                sum_xy = sum_xy + fit_x * composite[t]
            sums = jnp.where(lane == 4 * i + 2, lane_sum(sum_y), sums)
            sums = jnp.where(lane == 4 * i + 3, lane_sum(sum_xy), sums)
        return sums

    def sums_copy(peer):
        return pltpu.make_async_remote_copy(
            src_ref=part.at[peer],
            dst_ref=got.at[me],
            send_sem=send_b.at[peer],
            recv_sem=recv_b.at[me],
            device_id={AXIS: peer},
        )

    group = 8 if n % 8 == 0 else 1
    for top in range(n, 0, -group):
        peers = [me if spot == 0 else peer_at(spot) for spot in range(top - 1, top - group - 1, -1)]
        done = [finish(peer) for peer in peers]
        if top == group:
            sums = done.pop()
            peers.pop()
        for peer, value in zip(peers, done):
            part[peer] = value
        for peer in peers:
            sums_copy(peer).start()

    def take_sums(spot, total):
        source = peer_at(spot)
        pltpu.make_async_remote_copy(
            src_ref=part.at[source],
            dst_ref=got.at[source],
            send_sem=send_b.at[source],
            recv_sem=recv_b.at[source],
            device_id={AXIS: source},
        ).wait_recv()
        return total + got[source]

    sums = lax.fori_loop(1, n, take_sums, sums)
    weight_sum = sums[bands:, 0:1]
    for i in range(1, dates):
        weight_sum = jnp.where(lane >= 4 * i, sums[bands:, 4 * i:4 * i + 1], weight_sum)
    mean_x = sums / weight_sum
    mean_xx, mean_y, mean_xy = (pltpu.roll(mean_x, LANES - s, 1) for s in (1, 2, 3))
    gains = (mean_xy - mean_x * mean_y) / (mean_xx - mean_x * mean_x + 1e-5)
    offsets = mean_y - gains * mean_x
    for i in range(dates):
        gain = jnp.broadcast_to(gains[:, 4 * i:4 * i + 1], (rows, LANES))
        offset = jnp.broadcast_to(offsets[:, 4 * i:4 * i + 1], (rows, LANES))
        for b in range(bands):
            for h in range(halves):
                values = wide[i, h, b * tiles:(b + 1) * tiles]
                scaled = gain[b:b + 1] * values + offset[b:b + 1]
                out_ref[i, b, :, h * LANES:(h + 1) * LANES] = scaled.astype(out_ref.dtype)

    def drain(spot, carry):
        block_copy(peer_at(spot)).wait_send()
        sums_copy(peer_at(spot)).wait_send()
        return carry

    lax.fori_loop(1, n, drain, 0)


def local(n, scenes, quality, pif_mask, counts):
    scenes = scenes.transpose(0, 2, 1, 3)
    dates, bands, tiles, pix = scenes.shape
    mine = tiles // n
    rows = bands + 1
    in_place = pl.BlockSpec(memory_space=pltpu.HBM)
    out = pl.pallas_call(
        functools.partial(fused, n),
        out_shape=jax.ShapeDtypeStruct(scenes.shape, scenes.dtype),
        in_specs=[in_place] * 3 + [pl.BlockSpec(memory_space=pltpu.SMEM)],
        out_specs=pl.BlockSpec(memory_space=pltpu.VMEM),
        scratch_shapes=[
            pltpu.VMEM(scenes.shape, scenes.dtype),
            pltpu.VMEM(quality.shape, quality.dtype),
            pltpu.VMEM((dates, pix // LANES, rows * tiles, LANES), jnp.float32),
            pltpu.VMEM(pif_mask.shape, jnp.float32),
            pltpu.VMEM((tiles, dates, rows, pix), scenes.dtype),
            pltpu.VMEM((n, mine, dates, rows, pix), scenes.dtype),
            pltpu.VMEM((n, mine, dates, rows, pix), jnp.float32),
            pltpu.VMEM((n, rows, LANES), jnp.float32),
            pltpu.VMEM((n, rows, LANES), jnp.float32),
            pltpu.VMEM((n, rows, LANES), jnp.float32),
            pltpu.SemaphoreType.DMA((3,)),
            pltpu.SemaphoreType.DMA((n,)),
            pltpu.SemaphoreType.DMA((n,)),
            pltpu.SemaphoreType.DMA((n,)),
            pltpu.SemaphoreType.DMA((n,)),
        ],
        compiler_params=pltpu.CompilerParams(
            collective_id=0, has_side_effects=True, vmem_limit_bytes=32 * 2**20
        ),
    )(*(pltpu.with_memory_space_constraint(a, pltpu.HBM) for a in (scenes, quality, pif_mask)), counts)
    return out.transpose(0, 2, 1, 3)


def solution(mesh):
    both = ("groups", AXIS)
    placed = (P(both, None, None, None), P(both, None, None), P(both, None), P(both))
    return jax.shard_map(
        functools.partial(local, mesh.shape[AXIS]),
        mesh=mesh,
        in_specs=placed,
        out_specs=placed[0],
        check_vma=False,
    )
```

```python
import functools

import jax
import jax.numpy as jnp
from jax import lax
from jax.experimental import pallas as pl
from jax.experimental.pallas import tpu as pltpu
from jax.sharding import PartitionSpec as P

AXIS = "dates"
LANES = 128


def fused(n, scenes_hbm, quality_hbm, mask_hbm, counts_ref, out_ref,
          own, own_q, wide, mask, stage, recv, fitted, early, part, got,
          local_sem, send_a, recv_a, send_b, recv_b):
    dates, bands, tiles, pix = own.shape
    mine = tiles // n
    rows, halves = bands + 1, pix // LANES
    me = lax.axis_index(AXIS)

    barrier = pltpu.get_barrier_semaphore()

    def greet(k, carry):
        pl.semaphore_signal(barrier, inc=1, device_id={AXIS: lax.rem(me + k, n)})
        return carry

    lax.fori_loop(1, n, greet, 0)
    loads = [
        pltpu.make_async_copy(quality_hbm, own_q, local_sem.at[0]),
        pltpu.make_async_copy(scenes_hbm, own, local_sem.at[1]),
        pltpu.make_async_copy(mask_hbm, mask, local_sem.at[2]),
    ]
    for load in loads:
        load.start()
    for load in loads:
        load.wait()

    for i in range(dates):
        for h in range(halves):
            columns = slice(h * LANES, (h + 1) * LANES)
            for b in range(bands):
                wide[i, h, b * tiles:(b + 1) * tiles] = own[i, b, :, columns].astype(jnp.float32)
            wide[i, h, bands * tiles:] = own_q[i, :, columns].astype(jnp.float32)

    def stage_tile(t, carry):
        for i in range(dates):
            for h in range(halves):
                block = wide[i, h, pl.ds(t, rows, stride=tiles), :]
                stage[t, i, :, h * LANES:(h + 1) * LANES] = block.astype(jnp.bfloat16)
        return carry

    lax.fori_loop(0, tiles, stage_tile, 0, unroll=min(tiles, 16))
    recv[me] = stage[pl.ds(me * mine, mine)]

    pl.semaphore_wait(barrier, n - 1)

    def peer_at(spot):
        return lax.rem(me + spot, n)

    def source_at(spot):
        return lax.rem(me - spot + n, n)

    def block_copy(peer):
        return pltpu.make_async_remote_copy(
            src_ref=stage.at[pl.ds(peer * mine, mine)],
            dst_ref=recv.at[me],
            send_sem=send_a.at[peer],
            recv_sem=recv_a.at[me],
            device_id={AXIS: peer},
        )

    def block_arrival(source):
        return pltpu.make_async_remote_copy(
            src_ref=stage.at[pl.ds(source * mine, mine)],
            dst_ref=recv.at[source],
            send_sem=send_a.at[source],
            recv_sem=recv_a.at[source],
            device_id={AXIS: source},
        )

    def send_block(k, carry):
        block_copy(peer_at(k)).start()
        return carry

    lax.fori_loop(1, n, send_block, 0)

    last_row = lax.broadcasted_iota(jnp.int32, (rows, pix), 0) == bands
    lane = lax.broadcasted_iota(jnp.int32, (rows, LANES), 1)

    def lane_sum(values):
        return jnp.sum(values, axis=1, keepdims=True)

    def take(sources, totals):
        totals = list(totals)
        kept = []
        for source in sources:
            sums = jnp.zeros((rows, LANES), jnp.float32)
            parts = []
            for i in range(dates):
                sum_x = sum_xx = 0.0
                for t in range(mine):
                    block = recv[source, t, i].astype(jnp.float32)
                    covered = jnp.where(source * dates + i < counts_ref[t], 1.0, 0.0)
                    weight = block[bands:] * covered
                    values = jnp.where(last_row, 1.0, block)
                    weighted = weight * values
                    totals[t] = totals[t] + weighted
                    fit_x = weighted * mask[t:t + 1, :]
                    parts.append((t, i, fit_x))
                    sum_x = sum_x + fit_x
                    sum_xx = sum_xx + fit_x * values
                sums = jnp.where(lane == 4 * i, lane_sum(sum_x), sums)
                sums = jnp.where(lane == 4 * i + 1, lane_sum(sum_xx), sums)
            kept.append((source, sums, parts))
        for source, sums, parts in kept:
            early[source] = sums
            for t, i, fit_x in parts:
                fitted[source, t, i] = fit_x
        return tuple(totals)

    batch = 4 if n % 4 == 0 else 1
    totals = tuple(jnp.zeros((rows, pix), jnp.float32) for _ in range(mine))
    first = [source_at(spot) for spot in range(1, batch)]
    for source in first:
        block_arrival(source).wait_recv()
    totals = take([me] + first, totals)

    def take_batch(g, totals):
        sources = [source_at(g * batch + r) for r in range(batch)]
        for source in sources:
            block_arrival(source).wait_recv()
        return take(sources, totals)

    totals = lax.fori_loop(1, n // batch, take_batch, totals)
    composite = [total / total[bands:] for total in totals]

    def finish(source):
        sums = early[source]
        for i in range(dates):
            sum_y = sum_xy = 0.0
            for t in range(mine):
                fit_x = fitted[source, t, i]
                sum_y = sum_y + fit_x[bands:] * composite[t]
                sum_xy = sum_xy + fit_x * composite[t]
            sums = jnp.where(lane == 4 * i + 2, lane_sum(sum_y), sums)
            sums = jnp.where(lane == 4 * i + 3, lane_sum(sum_xy), sums)
        return sums

    def sums_copy(peer):
        return pltpu.make_async_remote_copy(
            src_ref=part.at[peer],
            dst_ref=got.at[me],
            send_sem=send_b.at[peer],
            recv_sem=recv_b.at[me],
            device_id={AXIS: peer},
        )

    group = 8 if n % 8 == 0 else 1
    for low in range(0, n, group):
        peers = [peer_at(low + r + 1) for r in range(group)]
        done = [finish(peer) for peer in peers]
        if low + group == n:
            sums = done.pop()
            peers.pop()
        for peer, value in zip(peers, done):
            part[peer] = value
        for peer in peers:
            sums_copy(peer).start()

    def take_sums(spot, total):
        source = source_at(spot)
        pltpu.make_async_remote_copy(
            src_ref=part.at[source],
            dst_ref=got.at[source],
            send_sem=send_b.at[source],
            recv_sem=recv_b.at[source],
            device_id={AXIS: source},
        ).wait_recv()
        return total + got[source]

    sums = lax.fori_loop(1, n, take_sums, sums)
    weight_sum = sums[bands:, 0:1]
    for i in range(1, dates):
        weight_sum = jnp.where(lane >= 4 * i, sums[bands:, 4 * i:4 * i + 1], weight_sum)
    mean_x = sums / weight_sum
    mean_xx, mean_y, mean_xy = (pltpu.roll(mean_x, LANES - s, 1) for s in (1, 2, 3))
    gains = (mean_xy - mean_x * mean_y) / (mean_xx - mean_x * mean_x + 1e-5)
    offsets = mean_y - gains * mean_x
    for i in range(dates):
        gain = jnp.broadcast_to(gains[:, 4 * i:4 * i + 1], (rows, LANES))
        offset = jnp.broadcast_to(offsets[:, 4 * i:4 * i + 1], (rows, LANES))
        for b in range(bands):
            for h in range(halves):
                values = wide[i, h, b * tiles:(b + 1) * tiles]
                scaled = gain[b:b + 1] * values + offset[b:b + 1]
                out_ref[i, b, :, h * LANES:(h + 1) * LANES] = scaled.astype(out_ref.dtype)

    def drain(spot, carry):
        block_copy(peer_at(spot)).wait_send()
        sums_copy(peer_at(spot)).wait_send()
        return carry

    lax.fori_loop(1, n, drain, 0)


def local(n, scenes, quality, pif_mask, counts):
    scenes = scenes.transpose(0, 2, 1, 3)
    dates, bands, tiles, pix = scenes.shape
    mine = tiles // n
    rows = bands + 1
    in_place = pl.BlockSpec(memory_space=pltpu.HBM)
    out = pl.pallas_call(
        functools.partial(fused, n),
        out_shape=jax.ShapeDtypeStruct(scenes.shape, scenes.dtype),
        in_specs=[in_place] * 3 + [pl.BlockSpec(memory_space=pltpu.SMEM)],
        out_specs=pl.BlockSpec(memory_space=pltpu.VMEM),
        scratch_shapes=[
            pltpu.VMEM(scenes.shape, scenes.dtype),
            pltpu.VMEM(quality.shape, quality.dtype),
            pltpu.VMEM((dates, pix // LANES, rows * tiles, LANES), jnp.float32),
            pltpu.VMEM(pif_mask.shape, jnp.float32),
            pltpu.VMEM((tiles, dates, rows, pix), scenes.dtype),
            pltpu.VMEM((n, mine, dates, rows, pix), scenes.dtype),
            pltpu.VMEM((n, mine, dates, rows, pix), jnp.float32),
            pltpu.VMEM((n, rows, LANES), jnp.float32),
            pltpu.VMEM((n, rows, LANES), jnp.float32),
            pltpu.VMEM((n, rows, LANES), jnp.float32),
            pltpu.SemaphoreType.DMA((3,)),
            pltpu.SemaphoreType.DMA((n,)),
            pltpu.SemaphoreType.DMA((n,)),
            pltpu.SemaphoreType.DMA((n,)),
            pltpu.SemaphoreType.DMA((n,)),
        ],
        compiler_params=pltpu.CompilerParams(
            collective_id=0, has_side_effects=True, vmem_limit_bytes=32 * 2**20
        ),
    )(*(pltpu.with_memory_space_constraint(a, pltpu.HBM) for a in (scenes, quality, pif_mask)), counts)
    return out.transpose(0, 2, 1, 3)


def solution(mesh):
    both = ("groups", AXIS)
    placed = (P(both, None, None, None), P(both, None, None), P(both, None), P(both))
    return jax.shard_map(
        functools.partial(local, mesh.shape[AXIS]),
        mesh=mesh,
        in_specs=placed,
        out_specs=placed[0],
        check_vma=False,
    )
```

```python
import functools

import jax
import jax.numpy as jnp
from jax import lax
from jax.experimental import pallas as pl
from jax.experimental.pallas import tpu as pltpu
from jax.sharding import PartitionSpec as P

AXIS = "dates"
LANES = 128


def fused(n, scenes_hbm, quality_hbm, mask_hbm, counts_ref, out_ref,
          own, own_q, wide, mask, stage, recv, fitted, early, part, got,
          local_sem, send_a, recv_a, send_b, recv_b):
    dates, bands, tiles, pix = own.shape
    mine = tiles // n
    rows, halves = bands + 1, pix // LANES
    me = lax.axis_index(AXIS)

    barrier = pltpu.get_barrier_semaphore()

    def greet(k, carry):
        pl.semaphore_signal(barrier, inc=1, device_id={AXIS: lax.rem(me + k, n)})
        return carry

    lax.fori_loop(1, n, greet, 0)
    loads = [
        pltpu.make_async_copy(quality_hbm, own_q, local_sem.at[0]),
        pltpu.make_async_copy(scenes_hbm, own, local_sem.at[1]),
        pltpu.make_async_copy(mask_hbm, mask, local_sem.at[2]),
    ]
    for load in loads:
        load.start()
    for load in loads:
        load.wait()

    for i in range(dates):
        for h in range(halves):
            columns = slice(h * LANES, (h + 1) * LANES)
            for b in range(bands):
                wide[i, h, b * tiles:(b + 1) * tiles] = own[i, b, :, columns].astype(jnp.float32)
            wide[i, h, bands * tiles:] = own_q[i, :, columns].astype(jnp.float32)

    def stage_tile(t, carry):
        for i in range(dates):
            for h in range(halves):
                block = wide[i, h, pl.ds(t, rows, stride=tiles), :]
                stage[t, i, :, h * LANES:(h + 1) * LANES] = block.astype(jnp.bfloat16)
        return carry

    lax.fori_loop(0, tiles, stage_tile, 0, unroll=min(tiles, 16))
    recv[me] = stage[pl.ds(me * mine, mine)]

    pl.semaphore_wait(barrier, n - 1)

    def peer_at(spot):
        return lax.rem(me + spot, n)

    def source_at(spot):
        return lax.rem(me - spot + n, n)

    def block_copy(peer):
        return pltpu.make_async_remote_copy(
            src_ref=stage.at[pl.ds(peer * mine, mine)],
            dst_ref=recv.at[me],
            send_sem=send_a.at[peer],
            recv_sem=recv_a.at[me],
            device_id={AXIS: peer},
        )

    def block_arrival(source):
        return pltpu.make_async_remote_copy(
            src_ref=stage.at[pl.ds(source * mine, mine)],
            dst_ref=recv.at[source],
            send_sem=send_a.at[source],
            recv_sem=recv_a.at[source],
            device_id={AXIS: source},
        )

    def send_block(k, carry):
        block_copy(peer_at(k)).start()
        return carry

    lax.fori_loop(1, n, send_block, 0)

    last_row = lax.broadcasted_iota(jnp.int32, (rows, pix), 0) == bands
    lane = lax.broadcasted_iota(jnp.int32, (rows, LANES), 1)
    width = 4 * dates
    base = width * bands
    slot = lane + width * lax.broadcasted_iota(jnp.int32, (rows, LANES), 0) - base

    def lane_sum(values):
        return jnp.sum(values, axis=1, keepdims=True)

    def take(sources, totals):
        totals = list(totals)
        kept = []
        for source in sources:
            sums = jnp.zeros((rows, LANES), jnp.float32)
            parts = []
            for i in range(dates):
                sum_x = sum_xx = 0.0
                for t in range(mine):
                    block = recv[source, t, i].astype(jnp.float32)
                    covered = jnp.where(source * dates + i < counts_ref[t], 1.0, 0.0)
                    weight = block[bands:] * covered
                    values = jnp.where(last_row, 1.0, block)
                    weighted = weight * values
                    totals[t] = totals[t] + weighted
                    fit_x = weighted * mask[t:t + 1, :]
                    parts.append((t, i, fit_x))
                    sum_x = sum_x + fit_x
                    sum_xx = sum_xx + fit_x * values
                sums = jnp.where(slot == 4 * i, lane_sum(sum_x), sums)
                sums = jnp.where(slot == 4 * i + 1, lane_sum(sum_xx), sums)
            kept.append((source, sums, parts))
        for source, sums, parts in kept:
            early[source] = sums
            for t, i, fit_x in parts:
                fitted[source, t, i] = fit_x
        return tuple(totals)

    batch = 4 if n % 4 == 0 else 1
    totals = tuple(jnp.zeros((rows, pix), jnp.float32) for _ in range(mine))
    first = [source_at(spot) for spot in range(1, batch)]
    for source in first:
        block_arrival(source).wait_recv()
    totals = take([me] + first, totals)

    def take_batch(g, totals):
        sources = [source_at(g * batch + r) for r in range(batch)]
        for source in sources:
            block_arrival(source).wait_recv()
        return take(sources, totals)

    totals = lax.fori_loop(1, n // batch, take_batch, totals)
    composite = [total / total[bands:] for total in totals]

    def finish(source):
        sums = early[source]
        for i in range(dates):
            sum_y = sum_xy = 0.0
            for t in range(mine):
                fit_x = fitted[source, t, i]
                sum_y = sum_y + fit_x[bands:] * composite[t]
                sum_xy = sum_xy + fit_x * composite[t]
            sums = jnp.where(slot == 4 * i + 2, lane_sum(sum_y), sums)
            sums = jnp.where(slot == 4 * i + 3, lane_sum(sum_xy), sums)
        return jnp.sum(sums, axis=0, keepdims=True)

    def sums_copy(peer):
        return pltpu.make_async_remote_copy(
            src_ref=part.at[peer],
            dst_ref=got.at[me],
            send_sem=send_b.at[peer],
            recv_sem=recv_b.at[me],
            device_id={AXIS: peer},
        )

    group = 8 if n % 8 == 0 else 1
    for low in range(0, n, group):
        peers = [peer_at(low + r + 1) for r in range(group)]
        done = [finish(peer) for peer in peers]
        if low + group == n:
            sums = done.pop()
            peers.pop()
        for peer, value in zip(peers, done):
            part[peer] = value
        for peer in peers:
            sums_copy(peer).start()

    def take_sums(spot, total):
        source = source_at(spot)
        pltpu.make_async_remote_copy(
            src_ref=part.at[source],
            dst_ref=got.at[source],
            send_sem=send_b.at[source],
            recv_sem=recv_b.at[source],
            device_id={AXIS: source},
        ).wait_recv()
        return total + got[source]

    sums = lax.fori_loop(1, n, take_sums, sums)
    sums = jnp.broadcast_to(sums, (rows, LANES))
    sums = pltpu.roll(sums, 0, 1, stride=width, stride_axis=0)
    weight_sum = sums[bands:, base:base + 1]
    for i in range(1, dates):
        weight_sum = jnp.where(lane >= base + 4 * i, sums[bands:, base + 4 * i:base + 4 * i + 1], weight_sum)
    mean_x = sums / weight_sum
    mean_xx, mean_y, mean_xy = (pltpu.roll(mean_x, LANES - s, 1) for s in (1, 2, 3))
    gains = (mean_xy - mean_x * mean_y) / (mean_xx - mean_x * mean_x + 1e-5)
    offsets = mean_y - gains * mean_x
    for i in range(dates):
        gain = jnp.broadcast_to(gains[:, base + 4 * i:base + 4 * i + 1], (rows, LANES))
        offset = jnp.broadcast_to(offsets[:, base + 4 * i:base + 4 * i + 1], (rows, LANES))
        for b in range(bands):
            for h in range(halves):
                values = wide[i, h, b * tiles:(b + 1) * tiles]
                scaled = gain[b:b + 1] * values + offset[b:b + 1]
                out_ref[i, b, :, h * LANES:(h + 1) * LANES] = scaled.astype(out_ref.dtype)

    def drain(spot, carry):
        block_copy(peer_at(spot)).wait_send()
        sums_copy(peer_at(spot)).wait_send()
        return carry

    lax.fori_loop(1, n, drain, 0)


def local(n, scenes, quality, pif_mask, counts):
    scenes = scenes.transpose(0, 2, 1, 3)
    dates, bands, tiles, pix = scenes.shape
    mine = tiles // n
    rows = bands + 1
    in_place = pl.BlockSpec(memory_space=pltpu.HBM)
    out = pl.pallas_call(
        functools.partial(fused, n),
        out_shape=jax.ShapeDtypeStruct(scenes.shape, scenes.dtype),
        in_specs=[in_place] * 3 + [pl.BlockSpec(memory_space=pltpu.SMEM)],
        out_specs=pl.BlockSpec(memory_space=pltpu.VMEM),
        scratch_shapes=[
            pltpu.VMEM(scenes.shape, scenes.dtype),
            pltpu.VMEM(quality.shape, quality.dtype),
            pltpu.VMEM((dates, pix // LANES, rows * tiles, LANES), jnp.float32),
            pltpu.VMEM(pif_mask.shape, jnp.float32),
            pltpu.VMEM((tiles, dates, rows, pix), scenes.dtype),
            pltpu.VMEM((n, mine, dates, rows, pix), scenes.dtype),
            pltpu.VMEM((n, mine, dates, rows, pix), jnp.float32),
            pltpu.VMEM((n, rows, LANES), jnp.float32),
            pltpu.VMEM((n, 1, LANES), jnp.float32),
            pltpu.VMEM((n, 1, LANES), jnp.float32),
            pltpu.SemaphoreType.DMA((3,)),
            pltpu.SemaphoreType.DMA((n,)),
            pltpu.SemaphoreType.DMA((n,)),
            pltpu.SemaphoreType.DMA((n,)),
            pltpu.SemaphoreType.DMA((n,)),
        ],
        compiler_params=pltpu.CompilerParams(
            collective_id=0, has_side_effects=True, vmem_limit_bytes=32 * 2**20
        ),
    )(*(pltpu.with_memory_space_constraint(a, pltpu.HBM) for a in (scenes, quality, pif_mask)), counts)
    return out.transpose(0, 2, 1, 3)


def solution(mesh):
    both = ("groups", AXIS)
    placed = (P(both, None, None, None), P(both, None, None), P(both, None), P(both))
    return jax.shard_map(
        functools.partial(local, mesh.shape[AXIS]),
        mesh=mesh,
        in_specs=placed,
        out_specs=placed[0],
        check_vma=False,
    )
```
